32 devices in a mesh: groups: 2 (over y), ctx: 4 (over z), chan: 4 (over x, core).
Axes of the slice: x: 2, y: 2, z: 4, core: 2. Of those that a mesh axis runs over, the one named last changes fastest.
Arguments:
- queries: bfloat16 [1024, 8192], P(('groups', 'ctx'), 'chan'), parts along dimension 0, may hold values from -6 to 6
- key_rows: bfloat16 [1024, 8192], P(('groups', 'ctx'), 'chan'), parts along dimension 0, may hold values from -6 to 6
- value_rows: bfloat16 [1024, 8192], P(('groups', 'ctx'), 'chan'), parts along dimension 0, may hold values from -6 to 6
- short_taps: float32 [3, 3, 8192], P(None, None, 'chan'), may hold values from -3 to 3
- bypass: float32 [8192], P('chan'), may hold values from -3 to 3
- decay_rate: float32 [512, 16], P('chan'), as said below
- residue: float32 [512, 16], P('chan'), may hold values from -3 to 3
- out_weight: bfloat16 [8192, 8192], P('ctx', 'chan'), may hold values from -0.0625 to 0.0625
- doc_lengths: int32 [16], P('groups'), parts along dimension 0, may hold values from 1 to 256, 512 in all
Outputs:
- layer_out: bfloat16 [1024, 8192], P(('groups', 'ctx'), 'chan'), parts along dimension 0
The draws below stay inside these ranges and needn't reach their ends.
There are 2 independent parts, one for each index of `groups`. The reference program is written for one: setup_inputs(seed, part) draws one part's arguments, and reference() takes and returns one part's arrays. A program takes and returns all parts, laid end to end along the dimension named above; an argument that names none is the same for every part. Nothing has to cross between parts.
Inputs may be any that keep to these rules, and one draw needn't show every extreme that they name: `doc_lengths`: the lengths sum to 512, and the longest is exactly 256. `decay_rate`: positive, at most 1 / 30.
All inputs are finite; a program needn't handle non-finite values.
Results may differ from the reference program's by a relative error of at most 0.0049.
Values may be sent and summed in bfloat16 or wider, within the bound.
A program may use at most 128 MiB of HBM per device.

```python
import math
import jax
import jax.numpy as jnp
import numpy as np
from jax import lax

D = 8192
MODES = 16
FILTERS = 512
DOCS = 8
SEQ = 512


def draw_decay_rate(key, part):
    second_key = jax.random.fold_in(jax.random.fold_in(key, 7), 1)
    level = jax.random.uniform(second_key, (FILTERS, MODES), jnp.float32)
    lowest = jnp.log(0.1 / SEQ)
    highest = jnp.log(1.0 / 30.0)
    return jnp.exp(lowest + level * (highest - lowest))


def steps_of(rng, extent, pieces, smallest, top_value):
    factor_of, own = 1.0, jax.random.fold_in(rng, 6)
    for dim, parts in pieces:
        draws = jnp.exp(jax.random.uniform(jax.random.fold_in(own, dim), (parts,), jnp.float32, smallest / len(pieces), top_value / len(pieces)))
        factor_of = factor_of * jnp.repeat(draws, extent[dim] // parts).reshape([-1 if axis == dim else 1 for axis in range(len(extent))])
    return factor_of


def split_up(number_of, total, reach, skew):
    loads = [(1 << 20) // math.isqrt(grade ** skew) + 1 for grade in range(2, number_of + 1)]
    surplus, counts = total - reach - (number_of - 1), [1] * (number_of - 1)
    while surplus > 0:
        movable = [i for i in range(number_of - 1) if counts[i] < reach]
        whole, left = sum([loads[i] for i in movable]), surplus
        for i in movable:
            extra = min(reach - counts[i], max(1, left * loads[i] // whole), surplus)
            counts[i] = counts[i] + extra
            surplus = surplus - extra
    return np.array([reach] + counts)


def ragged_sizes(key, number_of, total, limit, slope):
    if number_of == 2:
        one = jax.random.randint(key, (), max(1, total - limit), min(limit, total - 1) + 1)
        return jnp.stack([one, total - one])
    tallies = jnp.asarray(split_up(number_of, total, limit, slope), jnp.int32)
    twos = (number_of - 1) // 2
    donor, receiver = tallies[1:1 + 2 * twos:2], tallies[2:2 + 2 * twos:2]
    margin = jnp.minimum(donor - 1, limit - receiver)
    moved = jax.random.randint(jax.random.fold_in(key, 1), (twos,), 0, 1 << 20) % (margin + 1)
    tallies = tallies.at[1:1 + 2 * twos:2].set(donor - moved).at[2:2 + 2 * twos:2].set(receiver + moved)
    return tallies[jax.random.permutation(jax.random.fold_in(key, 2), number_of)]


def normal_values(rng, extent, deviation, bound, cuts=(), kind=jnp.bfloat16):
    array = deviation * jax.random.normal(rng, extent, jnp.float32)
    if cuts:
        array = array * steps_of(rng, extent, cuts, -0.22, 0.18)
    return jnp.clip(array, -bound, bound).astype(kind)


def setup_inputs(seed: int = 0, part: int = 0) -> dict:
    streams_of = jax.random.split(jax.random.key(seed), 10)
    part_keys = jax.random.split(jax.random.fold_in(streams_of[9], part), 10)
    queries = normal_values(part_keys[0], (SEQ, D), 1.0, 6.0, ((0, 4), (1, 4)))
    key_rows = normal_values(part_keys[1], (SEQ, D), 1.0, 6.0, ((0, 4), (1, 4)))
    value_rows = normal_values(part_keys[2], (SEQ, D), 1.0, 6.0, ((0, 4), (1, 4)))
    short_taps = normal_values(streams_of[3], (3, 3, D), 0.5, 3.0, ((2, 4),), jnp.float32)
    bypass = normal_values(streams_of[4], (D,), 0.5, 3.0, ((0, 4),), jnp.float32)
    decay_rate = draw_decay_rate(jax.random.fold_in(streams_of[9], 71), part)
    residue = normal_values(streams_of[6], (FILTERS, MODES), 0.5, 3.0, ((0, 4),), jnp.float32)
    out_weight = normal_values(streams_of[7], (D, D), D ** -0.5, 0.0625, ((0, 4), (1, 4)))
    doc_lengths = ragged_sizes(part_keys[8], DOCS, SEQ, SEQ // 2, 2).astype(jnp.int32)
    return dict(queries=queries, key_rows=key_rows, value_rows=value_rows, short_taps=short_taps, bypass=bypass, decay_rate=decay_rate, residue=residue, out_weight=out_weight, doc_lengths=doc_lengths)


def short_filter(values, taps):
    padded = jnp.pad(values.astype(jnp.float32), ((2, 0), (0, 0)))
    return taps[0] * padded[2:] + taps[1] * padded[1:-1] + taps[2] * padded[:-2]

def reference(queries, key_rows, value_rows, short_taps, bypass, decay_rate, residue, out_weight, doc_lengths):
    query_conv = short_filter(queries, short_taps[0])
    key_conv = short_filter(key_rows, short_taps[1])
    value_conv = short_filter(value_rows, short_taps[2])
    gated_input = key_conv * value_conv
    doc_starts = (jnp.cumsum(doc_lengths) - doc_lengths).astype(jnp.int32)
    positions = jnp.arange(SEQ, dtype=jnp.int32)
    docs = lax.optimization_barrier(jnp.sum((doc_starts[None, :] <= positions[:, None]).astype(jnp.int32), axis=1)) - 1
    keep_flag = jnp.concatenate([jnp.zeros((1,), jnp.float32), (docs[1:] == docs[:-1]).astype(jnp.float32)])
    group_size = D // FILTERS
    gain = residue * jnp.sqrt(-jnp.expm1(-2.0 * decay_rate))
    rate_chan = jnp.repeat(decay_rate, group_size, axis=0).T
    gain_chan = jnp.repeat(gain, group_size, axis=0).T
    factor = jnp.exp(-rate_chan)

    def advance(state, inputs):
        row, keep = inputs
        state = keep * factor * state + row[None, :]
        return (state, lax.optimization_barrier(jnp.sum(gain_chan * state, axis=0)))
    start_state = jnp.zeros((MODES, D), jnp.float32)
    _, conv = lax.scan(advance, start_state, (gated_input, keep_flag))
    mixed = (query_conv * (conv + bypass * gated_input)).astype(jnp.bfloat16)
    return jnp.dot(mixed, out_weight, preferred_element_type=jnp.float32).astype(jnp.bfloat16)
```

```python
import functools

import jax
import jax.numpy as jnp
from jax import lax
from jax.experimental import pallas as pl
from jax.experimental.pallas import tpu as pltpu
from jax.sharding import PartitionSpec as P

F32 = jnp.float32
BF16 = jnp.bfloat16
SIDE = 4
LANES = 512


def from_behind(value, axis, by):
    length = lax.axis_size(axis)
    pairs = [(i, i + by) for i in range(length) if 0 <= i + by < length]
    return lax.ppermute(value, axis, pairs)


def doc_index(doc_starts, positions):
    return jnp.sum((doc_starts[None, :] <= positions[:, None]).astype(jnp.int32), axis=1) - 1


def local(
    queries, key_rows, value_rows, short_taps, bypass, decay_rate, residue, out_weight, doc_lengths
):
    row_count, width_local = queries.shape
    filt_count, mode_count = decay_rate.shape
    group_size = width_local // filt_count
    dev_index = lax.axis_index("ctx")
    first_row = dev_index * row_count
    highest = lax.Precision.HIGHEST
    stacked = jnp.stack([queries, key_rows, value_rows])
    previous = from_behind(stacked[:, row_count - 2 :, :], "ctx", 1)
    extended = jnp.concatenate([previous, stacked], axis=1)
    filtered = (
        short_taps[:, 0, None, :] * extended[:, 2:, :]
        + short_taps[:, 1, None, :] * extended[:, 1:-1, :]
        + short_taps[:, 2, None, :] * extended[:, :-2, :]
    )
    query_conv = filtered[0]
    gated_input = filtered[1] * filtered[2]
    order = jnp.arange(doc_lengths.shape[0], dtype=jnp.int32)
    before = order[None, :] < order[:, None]
    doc_starts = jnp.sum(jnp.where(before, doc_lengths[None, :], 0), axis=1)
    own_positions = first_row - 1 + jnp.arange(row_count + 1, dtype=jnp.int32)
    docs_ext = doc_index(doc_starts, own_positions)
    doc_in = docs_ext[0]
    rate_t = decay_rate.T
    gain_t = (residue * jnp.sqrt(-jnp.expm1(-2.0 * decay_rate))).T
    block_len = min(128, row_count)
    lag_steps = jnp.arange(block_len, dtype=jnp.float32)
    lag_table = jnp.sum(
        gain_t[:, :, None] * jnp.exp(-rate_t[:, :, None] * lag_steps[None, None, :]), axis=0
    )
    lag_grid = jnp.arange(block_len)[:, None] - jnp.arange(block_len)[None, :]
    causal = lag_grid >= 0
    kernel = jnp.where(causal[None], lag_table[:, jnp.clip(lag_grid, 0, block_len - 1)], 0.0)
    end_weights = jnp.exp(-rate_t[:, :, None] * (block_len - 1.0 - lag_steps[None, None, :]))
    carry_table = gain_t[None, :, :] * jnp.exp(
        -rate_t[None, :, :] * (lag_steps[:, None, None] + 1.0)
    )
    full_decay = jnp.exp(-rate_t * block_len)
    local_starts = []
    local_state = jnp.zeros((mode_count, filt_count, group_size), jnp.float32)
    transfer = jnp.ones((mode_count, filt_count), jnp.float32)
    step = 0
    sub_rows = gated_input.reshape(block_len, filt_count, group_size)
    sub_docs = docs_ext[1 + step * block_len : 1 + (step + 1) * block_len]
    doc_before = docs_ext[step * block_len]
    same_doc = (sub_docs[:, None] == sub_docs[None, :]).astype(jnp.float32)
    masked = kernel * same_doc[None]
    intra_parts = [jnp.einsum("fij,jfg->ifg", masked, sub_rows, precision=highest)]
    last_mask = (sub_docs == sub_docs[-1]).astype(jnp.float32)
    end_state = jnp.einsum(
        "sfj,jfg->sfg", end_weights * last_mask[None, None, :], sub_rows, precision=highest
    )
    carry_masks = [(sub_docs == doc_before).astype(jnp.float32)]
    local_starts.append(local_state)
    transfer_starts = [transfer]
    step_decay = full_decay * (sub_docs[-1] == doc_before).astype(jnp.float32)
    local_state = step_decay[:, :, None] * local_state + end_state
    piece = lax.all_gather(local_state[None], "ctx", axis=0, tiled=True)
    count = piece.shape[0]
    source = jnp.arange(count, dtype=jnp.int32)
    end_docs = doc_index(doc_starts, (source + 1) * row_count - 1)
    valid = ((source < dev_index) & (end_docs == doc_in)).astype(jnp.float32)
    distance = jnp.maximum(dev_index - 1 - source, 0).astype(jnp.float32) * row_count
    factor = jnp.exp(-rate_t[None] * distance[:, None, None]) * valid[:, None, None]
    incoming = jnp.sum(factor[..., None] * piece, axis=0)
    step = 0
    state_start = transfer_starts[step][:, :, None] * incoming
    carried = jnp.einsum("isf,sfg->ifg", carry_table, state_start, precision=highest)
    total = intra_parts[step] + carried * carry_masks[step][:, None, None]
    conv_parts = total.reshape(block_len, width_local)
    mixed = (query_conv * (conv_parts + bypass * gated_input)).astype(jnp.bfloat16)
    weight_full = lax.all_gather(out_weight, "ctx", axis=0, tiled=True)
    projected = jnp.dot(
        lax.all_gather(mixed, "chan", axis=1, tiled=True),
        weight_full,
        preferred_element_type=jnp.float32,
    )
    return projected.astype(jnp.bfloat16)


def fused_kernel(
    docs_ref, q_hbm, k_hbm, v_hbm, taps_hbm, bypass_hbm, rates_ref, residues_ref, w_hbm, out_ref,
    q_ref, k_ref, v_ref, taps_ref, bypass_ref, in_sem,
    w_ref, halo_out, halo_in, ext, u_ref, um_ref, qc_ref, keep_ref, last_ref,
    rate_ref, gain_ref, fac_ref, e_out, e_in, st_ref, prod, mixed, hop_ref, lhs, part,
    own, hold, relay, recv,
    w_sem, halo_sem, e_send, e_recv, t_local, t_send, t_recv,
    hop_sem, x_send, x_recv, s_send, s_recv, rs_send, rs_recv, rl_recv,
):
    c = lax.axis_index("ctx")
    n = lax.axis_index("chan")
    rows, width = q_ref.shape
    modes = rate_ref.shape[0]
    group_size = width // rates_ref.shape[1]
    half = rows // 2
    sib = n + 1 - 2 * lax.rem(n, 2)
    opp = lax.rem(n + 2, SIDE)
    chunks = width // LANES

    def remote(src, dst, send, recv_sem, ctx, chan):
        return pltpu.make_async_remote_copy(
            src_ref=src, dst_ref=dst, send_sem=send, recv_sem=recv_sem,
            device_id={"ctx": ctx, "chan": chan}, device_id_type=pl.DeviceIdType.MESH,
        )

    loads = [
        pltpu.make_async_copy(src, dst, in_sem.at[i])
        for i, (src, dst) in enumerate(
            (
                (q_hbm, q_ref), (k_hbm, k_ref), (v_hbm, v_ref),
                (taps_hbm, taps_ref), (bypass_hbm, bypass_ref),
            )
        )
    ]
    for load in loads:
        load.start()
    load_w = pltpu.make_async_copy(w_hbm, w_ref, w_sem)
    load_w.start()

    barrier = pltpu.get_barrier_semaphore()

    def greet(ctx, chan):
        pl.semaphore_signal(
            barrier, inc=1, device_id={"ctx": ctx, "chan": chan},
            device_id_type=pl.DeviceIdType.MESH,
        )

    for j in range(1, SIDE):
        greet(lax.rem(c + j, SIDE), n)
        greet(c, lax.rem(n + j, SIDE))

    for load in loads:
        load.wait()
    for p, ref in enumerate((q_ref, k_ref, v_ref)):
        halo_out[2 * p : 2 * p + 2, :] = ref[rows - 16 :, :].astype(F32)[14:, :]
    halo_out[6:8, :] = jnp.zeros((2, width), F32)

    @pl.when(c == 0)
    def _():
        halo_in[...] = jnp.zeros_like(halo_in)
        e_in[0] = jnp.zeros_like(e_in[0])

    @pl.when(c <= 1)
    def _():
        e_in[1] = jnp.zeros_like(e_in[1])

    pl.semaphore_wait(barrier, 2 * SIDE - 2)

    halo = remote(halo_out, halo_in, halo_sem.at[0], halo_sem.at[1], lax.rem(c + 1, SIDE), n)

    @pl.when(c < SIDE - 1)
    def _():
        halo.start()

    first = c * rows
    pos = first + lax.broadcasted_iota(jnp.int32, (rows, 128), 0)
    keep = jnp.ones((rows, 128), F32)
    newest = jnp.int32(0)
    crossed = jnp.float32(1.0)
    start = jnp.int32(0)
    for j in range(docs_ref.shape[0]):
        keep = jnp.where(pos == start, 0.0, keep)
        newest = jnp.where(start < first + rows, start, newest)
        inside = jnp.logical_and(start >= first - rows, start < first)
        crossed = jnp.where(inside, jnp.float32(0.0), crossed)
        start = start + docs_ref[j]
    keep_ref[...] = keep
    last_ref[...] = jnp.where(pos >= newest, 1.0, 0.0)

    rate = rates_ref[...]
    twice = 2.0 * rate
    series = jnp.ones_like(twice)
    for term in range(8, 1, -1):
        series = 1.0 - twice * series * (1.0 / term)
    table = jnp.concatenate([rate, residues_ref[...] * jnp.sqrt(twice * series)], axis=0)

    def tables(i, carry):
        lanes = pl.ds(pl.multiple_of(i * LANES, LANES), LANES)
        filt = lax.broadcasted_iota(jnp.int32, (rates_ref.shape[1], LANES), 0)
        chan = lax.broadcasted_iota(jnp.int32, (rates_ref.shape[1], LANES), 1) + i * LANES
        pick = jnp.where(
            jnp.logical_and(chan >= filt * group_size, chan < (filt + 1) * group_size), 1.0, 0.0
        )
        both = jnp.dot(
            table, pick, precision=lax.Precision.HIGHEST, preferred_element_type=F32
        )
        rate_ref[:, lanes] = both[:modes]
        gain_ref[:, lanes] = both[modes:]
        fac_ref[:, lanes] = jnp.exp(-both[:modes])
        return carry

    lax.fori_loop(0, chunks, tables, 0)

    @pl.when(c > 0)
    def _():
        halo.wait_recv()

    def short(i, carry):
        lanes = pl.ds(pl.multiple_of(i * 128, 128), 128)
        convs = []
        for p, ref in enumerate((q_ref, k_ref, v_ref)):
            x = ref[:, lanes].astype(F32)
            ext[p, 8:, :] = x
            ext[p, 6:8, :] = halo_in[2 * p : 2 * p + 2, lanes]
            convs.append(
                taps_ref[p, 0:1, lanes] * x
                + taps_ref[p, 1:2, lanes] * ext[p, 7 : 7 + rows, :]
                + taps_ref[p, 2:3, lanes] * ext[p, 6 : 6 + rows, :]
            )
        u = convs[1] * convs[2]
        qc_ref[:, lanes] = convs[0]
        u_ref[:, lanes] = u
        um_ref[:, lanes] = u * last_ref[...]
        return carry

    lax.fori_loop(0, width // 128, short, 0)

    for part_no in range(2):
        for i in range(chunks // 2):
            at = (part_no * (chunks // 2) + i) * LANES
            lanes = slice(at, at + LANES)
            f0, f1 = fac_ref[0:8, lanes], fac_ref[8:16, lanes]

            def ends(t, state, lanes=lanes, f0=f0, f1=f1):
                s0, s1 = state
                for r in range(8):
                    row = jnp.broadcast_to(um_ref[pl.ds(t * 8 + r, 1), lanes], (8, LANES))
                    s0 = s0 * f0 + row
                    s1 = s1 * f1 + row
                return s0, s1

            zero = jnp.zeros((8, LANES), F32)
            s0, s1 = lax.fori_loop(0, rows // 8, ends, (zero, zero))
            e_out[part_no, :, i * LANES : (i + 1) * LANES] = jnp.concatenate([s0, s1]).astype(BF16)
        for d in range(2):

            @pl.when(c + d + 1 < SIDE)
            def _(d=d, part_no=part_no):
                remote(
                    e_out.at[part_no], e_in.at[d, part_no], e_send.at[d, part_no],
                    e_recv.at[d, part_no], lax.rem(c + d + 1, SIDE), n,
                ).start()

    for part_no in range(2):
        for d in range(2):

            @pl.when(c >= d + 1)
            def _(d=d, part_no=part_no):
                remote(
                    e_out.at[part_no], e_in.at[d, part_no], e_send.at[d, part_no],
                    e_recv.at[d, part_no], lax.rem(c + SIDE - d - 1, SIDE), n,
                ).wait_recv()

        part_width = width // 2
        lanes = slice(part_no * part_width, (part_no + 1) * part_width)
        st_ref[:, lanes] = e_in[0, part_no].astype(F32) + (crossed * e_in[1, part_no].astype(F32)) * jnp.exp(
            rate_ref[:, lanes] * (-1.0 * rows)
        )

    def scan_rows(h, first_group, groups):
        for i in range(chunks):
            lanes = slice(i * LANES, (i + 1) * LANES)
            f0, f1 = fac_ref[0:8, lanes], fac_ref[8:16, lanes]
            g0, g1 = gain_ref[0:8, lanes], gain_ref[8:16, lanes]

            def sweep(t, state, lanes=lanes, f0=f0, f1=f1, g0=g0, g1=g1):
                s0, s1 = state
                outs = []
                for b in range(2):
                    base = pl.multiple_of(h * half + first_group * 16 + t * 16 + b * 8, 8)
                    for r in range(8):
                        row = jnp.broadcast_to(u_ref[pl.ds(base + r, 1), lanes], (8, LANES))
                        kept = jnp.broadcast_to(keep_ref[pl.ds(base + r, 1), :], (8, 128))
                        kept = jnp.concatenate([kept] * (LANES // 128), axis=1)
                        s0 = (s0 * kept) * f0 + row
                        s1 = (s1 * kept) * f1 + row
                        terms = g0 * s0 + g1 * s1
                        for z in range(LANES // 128):
                            prod[b, z, r * 8 : r * 8 + 8, :] = terms[:, z * 128 : (z + 1) * 128]
                    sums = []
                    for z in range(LANES // 128):
                        acc = prod[b, z, pl.ds(0, 8, stride=8), :]
                        for m in range(1, 8):
                            acc = acc + prod[b, z, pl.ds(m, 8, stride=8), :]
                        sums.append(acc)
                    conv = jnp.concatenate(sums, axis=1)
                    outs.append(
                        qc_ref[pl.ds(base, 8), lanes]
                        * (conv + bypass_ref[:, lanes] * u_ref[pl.ds(base, 8), lanes])
                    )
                dest = pl.ds(pl.multiple_of(first_group * 16 + t * 16, 16), 16)
                mixed[h, dest, lanes] = jnp.concatenate(outs, axis=0).astype(BF16)
                return s0, s1

            s0, s1 = lax.fori_loop(0, groups, sweep, (st_ref[0:8, lanes], st_ref[8:16, lanes]))
            st_ref[0:8, lanes] = s0
            st_ref[8:16, lanes] = s1

    quarter = half // 2

    def piece(a):
        return slice(a * quarter, (a + 1) * quarter)

    def hop(a):
        return remote(
            mixed.at[0, piece(a)], hop_ref.at[piece(a)], hop_sem.at[a], hop_sem.at[2 + a], c, opp
        )

    def onward_hopped(a, plane):
        return remote(
            hop_ref.at[piece(a)], lhs.at[c, 0, piece(a)], t_send.at[a], t_recv.at[c], plane, n
        )

    def onward(plane):
        return remote(mixed.at[1], lhs.at[c, 1], t_send.at[2], t_recv.at[c], plane, n)

    def stay_hopped(a):
        return pltpu.make_async_copy(
            hop_ref.at[piece(a)], lhs.at[c, 0, piece(a)], t_local.at[a]
        )

    def stay():
        return pltpu.make_async_copy(mixed.at[1], lhs.at[c, 1], t_local.at[2])

    groups = half // 16
    scan_rows(0, 0, groups // 2)
    hop(0).start()
    scan_rows(0, groups // 2, groups - groups // 2)
    hop(1).start()
    scan_rows(1, 0, groups)

    @pl.when(n != c)
    def _():
        onward(n).start()

    @pl.when(n == c)
    def _():
        stay().start()

    for a in range(2):
        hop(a).wait_recv()

        @pl.when(opp != c)
        def _(a=a):
            onward_hopped(a, opp).start()

        @pl.when(opp == c)
        def _(a=a):
            stay_hopped(a).start()

    hub = lax.rem(n, 2) == lax.rem(c, 2)
    mine = jnp.where(n == c, 1, 0)
    theirs = 1 - mine

    def arrive(r, k):
        @pl.when(r != c)
        def _():
            remote(
                mixed.at[1], lhs.at[r, k], t_send.at[2], t_recv.at[r], lax.rem(c + 1, SIDE), n
            ).wait_recv()

        @pl.when(r == c)
        def _():
            if k == 1:
                stay().wait()
            else:
                stay_hopped(0).wait()
                stay_hopped(1).wait()

    def across(r, k):
        return remote(lhs.at[r, k], lhs.at[r, k], x_send.at[r], x_recv.at[r], c, opp)

    def hand(r, k):
        return remote(lhs.at[r, k], lhs.at[r, k], s_send.at[r, k], s_recv.at[r, k], c, sib)

    def pass_mine(r):
        @pl.when(hub)
        def _():
            @pl.when(n == c)
            def _():
                arrive(r, 1)

            @pl.when(n != c)
            def _():
                arrive(r, 0)

            across(r, mine).start()
            hand(r, mine).start()

    def pass_theirs(r):
        @pl.when(hub)
        def _():
            across(r, theirs).wait_recv()
            hand(r, theirs).start()

        @pl.when(jnp.logical_not(hub))
        def _():
            for k in range(2):
                hand(r, k).wait_recv()

    mate = c + 1 - 2 * lax.rem(c, 2)
    end = jnp.logical_or(c == 0, c == SIDE - 1)
    near = jnp.where(c < 2, 2, 1)
    away = jnp.where(c < 2, 3, 0)
    def direct(r, i):
        return remote(part.at[r, i], recv.at[0, i], rs_send.at[r, i], rs_recv.at[0, i], mate, n)

    def crossing(r, i):
        return remote(part.at[r, i], recv.at[1, i], rs_send.at[r, i], rs_recv.at[1, i], r, n)

    def to_relay(r, i):
        slot = lax.rem(r, 2)
        return remote(
            part.at[r, i], relay.at[slot, i], rs_send.at[r, i], rl_recv.at[slot, i], mate, n
        )

    def multiply(r):
        crosses = r // 2 != c // 2

        def tile(i, carry):
            cols = pl.ds(pl.multiple_of(i * LANES, LANES), LANES)
            acc = jnp.dot(
                lhs[r].reshape(rows, width), w_ref[:, cols], preferred_element_type=F32
            )

            @pl.when(r == c)
            def _():
                own[i] = acc

            @pl.when(jnp.logical_and(crosses, jnp.logical_not(end)))
            def _():
                hold[lax.rem(r, 2), i] = acc

            @pl.when(jnp.logical_and(crosses, end))
            def _():
                part[r, i] = acc.astype(BF16)
                to_relay(r, i).start()

            @pl.when(r == mate)
            def _():
                part[r, i] = acc.astype(BF16)
                direct(r, i).start()

            return carry

        lax.fori_loop(0, chunks, tile, 0)

    def add_relayed(r):
        @pl.when(jnp.logical_not(end))
        def _():
            slot = lax.rem(r, 2)

            def tile(i, carry):
                to_relay(r, i).wait_recv()
                part[r, i] = (hold[slot, i] + relay[slot, i].astype(F32)).astype(BF16)
                crossing(r, i).start()
                return carry

            lax.fori_loop(0, chunks, tile, 0)

    load_w.wait()
    pass_mine(c)
    pass_mine(mate)
    pass_theirs(c)
    multiply(c)
    pass_mine(near)
    pass_theirs(mate)
    multiply(mate)
    pass_mine(away)
    pass_theirs(near)
    multiply(near)
    pass_theirs(away)
    multiply(away)
    add_relayed(near)
    add_relayed(away)

    def finish(i, carry):
        cols = pl.ds(pl.multiple_of(i * LANES, LANES), LANES)
        direct(mate, i).wait_recv()
        total = own[i] + recv[0, i].astype(F32)
        remote(
            part.at[mate, i], recv.at[1, i], rs_send.at[mate, i], rs_recv.at[1, i], mate, n
        ).wait_recv()
        out_ref[:, cols] = (total + recv[1, i].astype(F32)).astype(BF16)
        return carry

    lax.fori_loop(0, chunks, finish, 0)

    @pl.when(c < SIDE - 1)
    def _():
        halo.wait_send()

    for part_no in range(2):
        for d in range(2):

            @pl.when(c + d + 1 < SIDE)
            def _(d=d, part_no=part_no):
                remote(
                    e_out.at[part_no], e_in.at[d, part_no], e_send.at[d, part_no],
                    e_recv.at[d, part_no], lax.rem(c + d + 1, SIDE), n,
                ).wait_send()

    hop(0).wait_send()
    hop(1).wait_send()

    @pl.when(n != c)
    def _():
        onward(n).wait_send()

    @pl.when(opp != c)
    def _():
        onward_hopped(0, opp).wait_send()
        onward_hopped(1, opp).wait_send()

    @pl.when(hub)
    def _():
        for r in range(SIDE):
            across(r, mine).wait_send()
            for k in range(2):
                hand(r, k).wait_send()

    for j in range(1, SIDE):

        def sent(i, carry, j=j):
            direct(lax.rem(c + j, SIDE), i).wait_send()
            return carry

        lax.fori_loop(0, chunks, sent, 0)


def fused(
    queries, key_rows, value_rows, short_taps, bypass, decay_rate, residue, out_weight, doc_lengths
):
    rows, width = queries.shape
    modes = decay_rate.shape[1]
    vmem = pl.BlockSpec(memory_space=pltpu.VMEM)
    hbm = pl.BlockSpec(memory_space=pltpu.HBM)
    tiles = width // LANES
    block = (rows, LANES)
    return pl.pallas_call(
        fused_kernel,
        out_shape=pltpu.VMEM((rows, width), BF16),
        in_specs=[pl.BlockSpec(memory_space=pltpu.SMEM)] + [hbm] * 5 + [vmem] * 2 + [hbm],
        out_specs=vmem,
        scratch_shapes=[
            pltpu.VMEM((rows, width), BF16),
            pltpu.VMEM((rows, width), BF16),
            pltpu.VMEM((rows, width), BF16),
            pltpu.VMEM((3, 3, width), F32),
            pltpu.VMEM((1, width), F32),
            pltpu.SemaphoreType.DMA((5,)),
            pltpu.VMEM(out_weight.shape, BF16),
            pltpu.VMEM((8, width), F32),
            pltpu.VMEM((8, width), F32),
            pltpu.VMEM((3, rows + 8, 128), F32),
            pltpu.VMEM((rows, width), F32),
            pltpu.VMEM((rows, width), F32),
            pltpu.VMEM((rows, width), F32),
            pltpu.VMEM((rows, 128), F32),
            pltpu.VMEM((rows, 128), F32),
            pltpu.VMEM((modes, width), F32),
            pltpu.VMEM((modes, width), F32),
            pltpu.VMEM((modes, width), F32),
            pltpu.VMEM((2, modes, width // 2), BF16),
            pltpu.VMEM((2, 2, modes, width // 2), BF16),
            pltpu.VMEM((modes, width), F32),
            pltpu.VMEM((2, LANES // 128, 64, 128), F32),
            pltpu.VMEM((2, rows // 2, width), BF16),
            pltpu.VMEM((rows // 2, width), BF16),
            pltpu.VMEM((SIDE, 2, rows // 2, width), BF16),
            pltpu.VMEM((SIDE, tiles) + block, BF16),
            pltpu.VMEM((tiles,) + block, F32),
            pltpu.VMEM((2, tiles) + block, F32),
            pltpu.VMEM((2, tiles) + block, BF16),
            pltpu.VMEM((2, tiles) + block, BF16),
            pltpu.SemaphoreType.DMA,
            pltpu.SemaphoreType.DMA((2,)),
            pltpu.SemaphoreType.DMA((2, 2)),
            pltpu.SemaphoreType.DMA((2, 2)),
            pltpu.SemaphoreType.DMA((3,)),
            pltpu.SemaphoreType.DMA((3,)),
            pltpu.SemaphoreType.DMA((SIDE,)),
            pltpu.SemaphoreType.DMA((4,)),
            pltpu.SemaphoreType.DMA((SIDE,)),
            pltpu.SemaphoreType.DMA((SIDE,)),
            pltpu.SemaphoreType.DMA((SIDE, 2)),
            pltpu.SemaphoreType.DMA((SIDE, 2)),
            pltpu.SemaphoreType.DMA((SIDE, tiles)),
            pltpu.SemaphoreType.DMA((2, tiles)),
            pltpu.SemaphoreType.DMA((2, tiles)),
        ],
        compiler_params=pltpu.CompilerParams(
            collective_id=0, has_side_effects=True, vmem_limit_bytes=62 << 20
        ),
    )(
        doc_lengths, queries, key_rows, value_rows, short_taps,
        bypass.reshape(1, width), decay_rate.T, residue.T, out_weight,
    )


def solution(mesh):
    square = mesh.shape["ctx"] == SIDE and mesh.shape["chan"] == SIDE
    return jax.shard_map(
        fused if square else local,
        mesh=mesh,
        in_specs=(
            P(("groups", "ctx"), "chan"),
            P(("groups", "ctx"), "chan"),
            P(("groups", "ctx"), "chan"),
            P(None, None, "chan"),
            P("chan"),
            P("chan", None),
            P("chan", None),
            P("ctx", "chan"),
            P("groups"),
        ),
        out_specs=P(("groups", "ctx"), "chan"),
        check_vma=False,
    )
```

```python
import functools

import jax
import jax.numpy as jnp
from jax import lax
from jax.experimental import pallas as pl
from jax.experimental.pallas import tpu as pltpu
from jax.sharding import PartitionSpec as P

F32 = jnp.float32
BF16 = jnp.bfloat16
SIDE = 4
LANES = 512


def from_behind(value, axis, by):
    length = lax.axis_size(axis)
    pairs = [(i, i + by) for i in range(length) if 0 <= i + by < length]
    return lax.ppermute(value, axis, pairs)


def doc_index(doc_starts, positions):
    return jnp.sum((doc_starts[None, :] <= positions[:, None]).astype(jnp.int32), axis=1) - 1


def local(
    queries, key_rows, value_rows, short_taps, bypass, decay_rate, residue, out_weight, doc_lengths
):
    row_count, width_local = queries.shape
    filt_count, mode_count = decay_rate.shape
    group_size = width_local // filt_count
    dev_index = lax.axis_index("ctx")
    first_row = dev_index * row_count
    highest = lax.Precision.HIGHEST
    stacked = jnp.stack([queries, key_rows, value_rows])
    previous = from_behind(stacked[:, row_count - 2 :, :], "ctx", 1)
    extended = jnp.concatenate([previous, stacked], axis=1)
    filtered = (
        short_taps[:, 0, None, :] * extended[:, 2:, :]
        + short_taps[:, 1, None, :] * extended[:, 1:-1, :]
        + short_taps[:, 2, None, :] * extended[:, :-2, :]
    )
    query_conv = filtered[0]
    gated_input = filtered[1] * filtered[2]
    order = jnp.arange(doc_lengths.shape[0], dtype=jnp.int32)
    before = order[None, :] < order[:, None]
    doc_starts = jnp.sum(jnp.where(before, doc_lengths[None, :], 0), axis=1)
    own_positions = first_row - 1 + jnp.arange(row_count + 1, dtype=jnp.int32)
    docs_ext = doc_index(doc_starts, own_positions)
    doc_in = docs_ext[0]
    rate_t = decay_rate.T
    gain_t = (residue * jnp.sqrt(-jnp.expm1(-2.0 * decay_rate))).T
    block_len = min(128, row_count)
    lag_steps = jnp.arange(block_len, dtype=jnp.float32)
    lag_table = jnp.sum(
        gain_t[:, :, None] * jnp.exp(-rate_t[:, :, None] * lag_steps[None, None, :]), axis=0
    )
    lag_grid = jnp.arange(block_len)[:, None] - jnp.arange(block_len)[None, :]
    causal = lag_grid >= 0
    kernel = jnp.where(causal[None], lag_table[:, jnp.clip(lag_grid, 0, block_len - 1)], 0.0)
    end_weights = jnp.exp(-rate_t[:, :, None] * (block_len - 1.0 - lag_steps[None, None, :]))
    carry_table = gain_t[None, :, :] * jnp.exp(
        -rate_t[None, :, :] * (lag_steps[:, None, None] + 1.0)
    )
    full_decay = jnp.exp(-rate_t * block_len)
    local_starts = []
    local_state = jnp.zeros((mode_count, filt_count, group_size), jnp.float32)
    transfer = jnp.ones((mode_count, filt_count), jnp.float32)
    step = 0
    sub_rows = gated_input.reshape(block_len, filt_count, group_size)
    sub_docs = docs_ext[1 + step * block_len : 1 + (step + 1) * block_len]
    doc_before = docs_ext[step * block_len]
    same_doc = (sub_docs[:, None] == sub_docs[None, :]).astype(jnp.float32)
    masked = kernel * same_doc[None]
    intra_parts = [jnp.einsum("fij,jfg->ifg", masked, sub_rows, precision=highest)]
    last_mask = (sub_docs == sub_docs[-1]).astype(jnp.float32)
    end_state = jnp.einsum(
        "sfj,jfg->sfg", end_weights * last_mask[None, None, :], sub_rows, precision=highest
    )
    carry_masks = [(sub_docs == doc_before).astype(jnp.float32)]
    local_starts.append(local_state)
    transfer_starts = [transfer]
    step_decay = full_decay * (sub_docs[-1] == doc_before).astype(jnp.float32)
    local_state = step_decay[:, :, None] * local_state + end_state
    piece = lax.all_gather(local_state[None], "ctx", axis=0, tiled=True)
    count = piece.shape[0]
    source = jnp.arange(count, dtype=jnp.int32)
    end_docs = doc_index(doc_starts, (source + 1) * row_count - 1)
    valid = ((source < dev_index) & (end_docs == doc_in)).astype(jnp.float32)
    distance = jnp.maximum(dev_index - 1 - source, 0).astype(jnp.float32) * row_count
    factor = jnp.exp(-rate_t[None] * distance[:, None, None]) * valid[:, None, None]
    incoming = jnp.sum(factor[..., None] * piece, axis=0)
    step = 0
    state_start = transfer_starts[step][:, :, None] * incoming
    carried = jnp.einsum("isf,sfg->ifg", carry_table, state_start, precision=highest)
    total = intra_parts[step] + carried * carry_masks[step][:, None, None]
    conv_parts = total.reshape(block_len, width_local)
    mixed = (query_conv * (conv_parts + bypass * gated_input)).astype(jnp.bfloat16)
    weight_full = lax.all_gather(out_weight, "ctx", axis=0, tiled=True)
    projected = jnp.dot(
        lax.all_gather(mixed, "chan", axis=1, tiled=True),
        weight_full,
        preferred_element_type=jnp.float32,
    )
    return projected.astype(jnp.bfloat16)


def fused_kernel(
    docs_ref, q_hbm, k_hbm, v_hbm, taps_hbm, bypass_hbm, rates_ref, residues_ref, w_hbm, out_ref,
    q_ref, k_ref, v_ref, taps_ref, bypass_ref, in_sem,
    w_ref, halo_out, halo_in, ext, u_ref, um_ref, qc_ref, keep_ref, last_ref,
    rate_ref, gain_ref, fac_ref, e_out, e_in, st_ref, prod, mixed, hop_ref, lhs, part,
    own, hold, relay, recv,
    w_sem, halo_sem, e_send, e_recv, t_local, t_send, t_recv,
    hop_sem, x_send, x_recv, s_send, s_recv, rs_send, rs_recv, rl_recv,
):
    c = lax.axis_index("ctx")
    n = lax.axis_index("chan")
    rows, width = q_ref.shape
    modes = rate_ref.shape[0]
    group_size = width // rates_ref.shape[1]
    half = rows // 2
    sib = n + 1 - 2 * lax.rem(n, 2)
    opp = lax.rem(n + 2, SIDE)
    chunks = width // LANES

    def remote(src, dst, send, recv_sem, ctx, chan):
        return pltpu.make_async_remote_copy(
            src_ref=src, dst_ref=dst, send_sem=send, recv_sem=recv_sem,
            device_id={"ctx": ctx, "chan": chan}, device_id_type=pl.DeviceIdType.MESH,
        )

    loads = [
        pltpu.make_async_copy(src, dst, in_sem.at[i])
        for i, (src, dst) in enumerate(
            (
                (q_hbm, q_ref), (k_hbm, k_ref), (v_hbm, v_ref),
                (taps_hbm, taps_ref), (bypass_hbm, bypass_ref),
            )
        )
    ]
    for load in loads:
        load.start()
    load_w = pltpu.make_async_copy(w_hbm, w_ref, w_sem)
    load_w.start()

    barrier = pltpu.get_barrier_semaphore()

    def greet(ctx, chan):
        pl.semaphore_signal(
            barrier, inc=1, device_id={"ctx": ctx, "chan": chan},
            device_id_type=pl.DeviceIdType.MESH,
        )

    for j in range(1, SIDE):
        greet(lax.rem(c + j, SIDE), n)
        greet(c, lax.rem(n + j, SIDE))

    for load in loads:
        load.wait()
    for p, ref in enumerate((q_ref, k_ref, v_ref)):
        halo_out[2 * p : 2 * p + 2, :] = ref[rows - 16 :, :].astype(F32)[14:, :]
    halo_out[6:8, :] = jnp.zeros((2, width), F32)

    @pl.when(c == 0)
    def _():
        halo_in[...] = jnp.zeros_like(halo_in)
        e_in[0] = jnp.zeros_like(e_in[0])

    @pl.when(c <= 1)
    def _():
        e_in[1] = jnp.zeros_like(e_in[1])

    pl.semaphore_wait(barrier, 2 * SIDE - 2)

    halo = remote(halo_out, halo_in, halo_sem.at[0], halo_sem.at[1], lax.rem(c + 1, SIDE), n)

    @pl.when(c < SIDE - 1)
    def _():
        halo.start()

    first = c * rows
    pos = first + lax.broadcasted_iota(jnp.int32, (rows, 128), 0)
    keep = jnp.ones((rows, 128), F32)
    newest = jnp.int32(0)
    crossed = jnp.float32(1.0)
    start = jnp.int32(0)
    for j in range(docs_ref.shape[0]):
        keep = jnp.where(pos == start, 0.0, keep)
        newest = jnp.where(start < first + rows, start, newest)
        inside = jnp.logical_and(start >= first - rows, start < first)
        crossed = jnp.where(inside, jnp.float32(0.0), crossed)
        start = start + docs_ref[j]
    keep_ref[...] = keep
    last_ref[...] = jnp.where(pos >= newest, 1.0, 0.0)

    rate = rates_ref[...]
    twice = 2.0 * rate
    series = jnp.ones_like(twice)
    for term in range(8, 1, -1):
        series = 1.0 - twice * series * (1.0 / term)
    table = jnp.concatenate([rate, residues_ref[...] * jnp.sqrt(twice * series)], axis=0)

    def tables(i, carry):
        lanes = pl.ds(pl.multiple_of(i * LANES, LANES), LANES)
        filt = lax.broadcasted_iota(jnp.int32, (rates_ref.shape[1], LANES), 0)
        chan = lax.broadcasted_iota(jnp.int32, (rates_ref.shape[1], LANES), 1) + i * LANES
        pick = jnp.where(
            jnp.logical_and(chan >= filt * group_size, chan < (filt + 1) * group_size), 1.0, 0.0
        )
        both = jnp.dot(
            table, pick, precision=lax.Precision.HIGHEST, preferred_element_type=F32
        )
        rate_ref[:, lanes] = both[:modes]
        gain_ref[:, lanes] = both[modes:]
        fac_ref[:, lanes] = jnp.exp(-both[:modes])
        return carry

    lax.fori_loop(0, chunks, tables, 0)

    @pl.when(c > 0)
    def _():
        halo.wait_recv()

    def short(i, carry):
        lanes = pl.ds(pl.multiple_of(i * 128, 128), 128)
        convs = []
        for p, ref in enumerate((q_ref, k_ref, v_ref)):
            x = ref[:, lanes].astype(F32)
            ext[p, 8:, :] = x
            ext[p, 6:8, :] = halo_in[2 * p : 2 * p + 2, lanes]
            convs.append(
                taps_ref[p, 0:1, lanes] * x
                + taps_ref[p, 1:2, lanes] * ext[p, 7 : 7 + rows, :]
                + taps_ref[p, 2:3, lanes] * ext[p, 6 : 6 + rows, :]
            )
        u = convs[1] * convs[2]
        qc_ref[:, lanes] = convs[0]
        u_ref[:, lanes] = u
        um_ref[:, lanes] = u * last_ref[...]
        return carry

    lax.fori_loop(0, width // 128, short, 0)

    for part_no in range(2):
        for i in range(chunks // 2):
            at = (part_no * (chunks // 2) + i) * LANES
            lanes = slice(at, at + LANES)
            f0, f1 = fac_ref[0:8, lanes], fac_ref[8:16, lanes]

            def ends(t, state, lanes=lanes, f0=f0, f1=f1):
                s0, s1 = state
                for r in range(8):
                    row = jnp.broadcast_to(um_ref[pl.ds(t * 8 + r, 1), lanes], (8, LANES))
                    s0 = s0 * f0 + row
                    s1 = s1 * f1 + row
                return s0, s1

            zero = jnp.zeros((8, LANES), F32)
            s0, s1 = lax.fori_loop(0, rows // 8, ends, (zero, zero))
            e_out[part_no, :, i * LANES : (i + 1) * LANES] = jnp.concatenate([s0, s1]).astype(BF16)
        for d in range(2):

            @pl.when(c + d + 1 < SIDE)
            def _(d=d, part_no=part_no):
                remote(
                    e_out.at[part_no], e_in.at[d, part_no], e_send.at[d, part_no],
                    e_recv.at[d, part_no], lax.rem(c + d + 1, SIDE), n,
                ).start()

    for part_no in range(2):
        for d in range(2):

            @pl.when(c >= d + 1)
            def _(d=d, part_no=part_no):
                remote(
                    e_out.at[part_no], e_in.at[d, part_no], e_send.at[d, part_no],
                    e_recv.at[d, part_no], lax.rem(c + SIDE - d - 1, SIDE), n,
                ).wait_recv()

        part_width = width // 2
        lanes = slice(part_no * part_width, (part_no + 1) * part_width)
        st_ref[:, lanes] = e_in[0, part_no].astype(F32) + (crossed * e_in[1, part_no].astype(F32)) * jnp.exp(
            rate_ref[:, lanes] * (-1.0 * rows)
        )

    def scan_rows(h, first_group, groups):
        for i in range(chunks):
            lanes = slice(i * LANES, (i + 1) * LANES)
            f0, f1 = fac_ref[0:8, lanes], fac_ref[8:16, lanes]
            g0, g1 = gain_ref[0:8, lanes], gain_ref[8:16, lanes]

            def sweep(t, state, lanes=lanes, f0=f0, f1=f1, g0=g0, g1=g1):
                s0, s1 = state
                outs = []
                for b in range(2):
                    base = pl.multiple_of(h * half + first_group * 16 + t * 16 + b * 8, 8)
                    for r in range(8):
                        row = jnp.broadcast_to(u_ref[pl.ds(base + r, 1), lanes], (8, LANES))
                        kept = jnp.broadcast_to(keep_ref[pl.ds(base + r, 1), :], (8, 128))
                        kept = jnp.concatenate([kept] * (LANES // 128), axis=1)
                        s0 = (s0 * kept) * f0 + row
                        s1 = (s1 * kept) * f1 + row
                        terms = g0 * s0 + g1 * s1
                        for z in range(LANES // 128):
                            prod[b, z, r * 8 : r * 8 + 8, :] = terms[:, z * 128 : (z + 1) * 128]
                    sums = []
                    for z in range(LANES // 128):
                        acc = prod[b, z, pl.ds(0, 8, stride=8), :]
                        for m in range(1, 8):
                            acc = acc + prod[b, z, pl.ds(m, 8, stride=8), :]
                        sums.append(acc)
                    conv = jnp.concatenate(sums, axis=1)
                    outs.append(
                        qc_ref[pl.ds(base, 8), lanes]
                        * (conv + bypass_ref[:, lanes] * u_ref[pl.ds(base, 8), lanes])
                    )
                dest = pl.ds(pl.multiple_of(first_group * 16 + t * 16, 16), 16)
                mixed[h, dest, lanes] = jnp.concatenate(outs, axis=0).astype(BF16)
                return s0, s1

            s0, s1 = lax.fori_loop(0, groups, sweep, (st_ref[0:8, lanes], st_ref[8:16, lanes]))
            st_ref[0:8, lanes] = s0
            st_ref[8:16, lanes] = s1

    quarter = half // 2

    def piece(a):
        return slice(a * quarter, (a + 1) * quarter)

    def hop(a):
        return remote(
            mixed.at[0, piece(a)], hop_ref.at[piece(a)], hop_sem.at[a], hop_sem.at[2 + a], c, opp
        )

    def onward_hopped(a, plane):
        return remote(
            hop_ref.at[piece(a)], lhs.at[c, 0, piece(a)], t_send.at[a], t_recv.at[c], plane, n
        )

    def onward(plane):
        return remote(mixed.at[1], lhs.at[c, 1], t_send.at[2], t_recv.at[c], plane, n)

    def stay_hopped(a):
        return pltpu.make_async_copy(
            hop_ref.at[piece(a)], lhs.at[c, 0, piece(a)], t_local.at[a]
        )

    def stay():
        return pltpu.make_async_copy(mixed.at[1], lhs.at[c, 1], t_local.at[2])

    groups = half // 16
    scan_rows(0, 0, groups // 2)
    hop(0).start()
    scan_rows(0, groups // 2, groups - groups // 2)
    hop(1).start()
    scan_rows(1, 0, groups)

    @pl.when(n != c)
    def _():
        onward(n).start()

    @pl.when(n == c)
    def _():
        stay().start()

    for a in range(2):
        hop(a).wait_recv()

        @pl.when(opp != c)
        def _(a=a):
            onward_hopped(a, opp).start()

        @pl.when(opp == c)
        def _(a=a):
            stay_hopped(a).start()

    hub = lax.rem(n, 2) == lax.rem(c, 2)
    mine = jnp.where(n == c, 1, 0)
    theirs = 1 - mine

    def arrive(r, k):
        @pl.when(r != c)
        def _():
            remote(
                mixed.at[1], lhs.at[r, k], t_send.at[2], t_recv.at[r], lax.rem(c + 1, SIDE), n
            ).wait_recv()

        @pl.when(r == c)
        def _():
            if k == 1:
                stay().wait()
            else:
                stay_hopped(0).wait()
                stay_hopped(1).wait()

    def across(r, k):
        return remote(lhs.at[r, k], lhs.at[r, k], x_send.at[r], x_recv.at[r], c, opp)

    def hand(r, k):
        return remote(lhs.at[r, k], lhs.at[r, k], s_send.at[r, k], s_recv.at[r, k], c, sib)

    def pass_mine(r):
        @pl.when(hub)
        def _():
            @pl.when(n == c)
            def _():
                arrive(r, 1)

            @pl.when(n != c)
            def _():
                arrive(r, 0)

            across(r, mine).start()
            hand(r, mine).start()

    def pass_theirs(r):
        @pl.when(hub)
        def _():
            across(r, theirs).wait_recv()
            hand(r, theirs).start()

        @pl.when(jnp.logical_not(hub))
        def _():
            for k in range(2):
                hand(r, k).wait_recv()

    mate = c + 1 - 2 * lax.rem(c, 2)
    end = jnp.logical_or(c == 0, c == SIDE - 1)
    near = jnp.where(c < 2, 2, 1)
    away = jnp.where(c < 2, 3, 0)
    def direct(r, i):
        return remote(part.at[r, i], recv.at[0, i], rs_send.at[r, i], rs_recv.at[0, i], mate, n)

    def crossing(r, i):
        return remote(part.at[r, i], recv.at[1, i], rs_send.at[r, i], rs_recv.at[1, i], r, n)

    def to_relay(r, i):
        slot = lax.rem(r, 2)
        return remote(
            part.at[r, i], relay.at[slot, i], rs_send.at[r, i], rl_recv.at[slot, i], mate, n
        )

    def multiply(r):
        crosses = r // 2 != c // 2

        def tile(i, carry):
            cols = pl.ds(pl.multiple_of(i * LANES, LANES), LANES)
            acc = jnp.dot(
                lhs[r].reshape(rows, width), w_ref[:, cols], preferred_element_type=F32
            )

            @pl.when(r == c)
            def _():
                own[i] = acc

            @pl.when(jnp.logical_and(crosses, jnp.logical_not(end)))
            def _():
                hold[lax.rem(r, 2), i] = acc

            @pl.when(jnp.logical_and(crosses, end))
            def _():
                part[r, i] = acc.astype(BF16)
                to_relay(r, i).start()

            @pl.when(r == mate)
            def _():
                part[r, i] = acc.astype(BF16)

                @pl.when(jnp.logical_or(jnp.logical_not(end), i < 2))
                def _():
                    direct(r, i).start()

            return carry

        lax.fori_loop(0, chunks, tile, 0)

    def add_relayed(r):
        @pl.when(jnp.logical_not(end))
        def _():
            slot = lax.rem(r, 2)

            def tile(i, carry):
                to_relay(r, i).wait_recv()
                part[r, i] = (hold[slot, i] + relay[slot, i].astype(F32)).astype(BF16)
                crossing(r, i).start()
                return carry

            lax.fori_loop(0, chunks, tile, 0)

    load_w.wait()
    pass_mine(c)
    pass_mine(mate)
    pass_theirs(c)
    multiply(c)
    pass_mine(away)
    pass_theirs(mate)
    multiply(mate)
    pass_mine(near)
    pass_theirs(away)
    multiply(away)
    pass_theirs(near)
    multiply(near)

    @pl.when(end)
    def _():
        for i in range(2, chunks):
            direct(mate, i).start()

    add_relayed(away)
    add_relayed(near)

    def finish(i, carry):
        cols = pl.ds(pl.multiple_of(i * LANES, LANES), LANES)
        direct(mate, i).wait_recv()
        total = own[i] + recv[0, i].astype(F32)
        remote(
            part.at[mate, i], recv.at[1, i], rs_send.at[mate, i], rs_recv.at[1, i], mate, n
        ).wait_recv()
        out_ref[:, cols] = (total + recv[1, i].astype(F32)).astype(BF16)
        return carry

    lax.fori_loop(0, chunks, finish, 0)

    @pl.when(c < SIDE - 1)
    def _():
        halo.wait_send()

    for part_no in range(2):
        for d in range(2):

            @pl.when(c + d + 1 < SIDE)
            def _(d=d, part_no=part_no):
                remote(
                    e_out.at[part_no], e_in.at[d, part_no], e_send.at[d, part_no],
                    e_recv.at[d, part_no], lax.rem(c + d + 1, SIDE), n,
                ).wait_send()

    hop(0).wait_send()
    hop(1).wait_send()

    @pl.when(n != c)
    def _():
        onward(n).wait_send()

    @pl.when(opp != c)
    def _():
        onward_hopped(0, opp).wait_send()
        onward_hopped(1, opp).wait_send()

    @pl.when(hub)
    def _():
        for r in range(SIDE):
            across(r, mine).wait_send()
            for k in range(2):
                hand(r, k).wait_send()

    for j in range(1, SIDE):

        def sent(i, carry, j=j):
            direct(lax.rem(c + j, SIDE), i).wait_send()
            return carry

        lax.fori_loop(0, chunks, sent, 0)


def fused(
    queries, key_rows, value_rows, short_taps, bypass, decay_rate, residue, out_weight, doc_lengths
):
    rows, width = queries.shape
    modes = decay_rate.shape[1]
    vmem = pl.BlockSpec(memory_space=pltpu.VMEM)
    hbm = pl.BlockSpec(memory_space=pltpu.HBM)
    tiles = width // LANES
    block = (rows, LANES)
    return pl.pallas_call(
        fused_kernel,
        out_shape=pltpu.VMEM((rows, width), BF16),
        in_specs=[pl.BlockSpec(memory_space=pltpu.SMEM)] + [hbm] * 5 + [vmem] * 2 + [hbm],
        out_specs=vmem,
        scratch_shapes=[
            pltpu.VMEM((rows, width), BF16),
            pltpu.VMEM((rows, width), BF16),
            pltpu.VMEM((rows, width), BF16),
            pltpu.VMEM((3, 3, width), F32),
            pltpu.VMEM((1, width), F32),
            pltpu.SemaphoreType.DMA((5,)),
            pltpu.VMEM(out_weight.shape, BF16),
            pltpu.VMEM((8, width), F32),
            pltpu.VMEM((8, width), F32),
            pltpu.VMEM((3, rows + 8, 128), F32),
            pltpu.VMEM((rows, width), F32),
            pltpu.VMEM((rows, width), F32),
            pltpu.VMEM((rows, width), F32),
            pltpu.VMEM((rows, 128), F32),
            pltpu.VMEM((rows, 128), F32),
            pltpu.VMEM((modes, width), F32),
            pltpu.VMEM((modes, width), F32),
            pltpu.VMEM((modes, width), F32),
            pltpu.VMEM((2, modes, width // 2), BF16),
            pltpu.VMEM((2, 2, modes, width // 2), BF16),
            pltpu.VMEM((modes, width), F32),
            pltpu.VMEM((2, LANES // 128, 64, 128), F32),
            pltpu.VMEM((2, rows // 2, width), BF16),
            pltpu.VMEM((rows // 2, width), BF16),
            pltpu.VMEM((SIDE, 2, rows // 2, width), BF16),
            pltpu.VMEM((SIDE, tiles) + block, BF16),
            pltpu.VMEM((tiles,) + block, F32),
            pltpu.VMEM((2, tiles) + block, F32),
            pltpu.VMEM((2, tiles) + block, BF16),
            pltpu.VMEM((2, tiles) + block, BF16),
            pltpu.SemaphoreType.DMA,
            pltpu.SemaphoreType.DMA((2,)),
            pltpu.SemaphoreType.DMA((2, 2)),
            pltpu.SemaphoreType.DMA((2, 2)),
            pltpu.SemaphoreType.DMA((3,)),
            pltpu.SemaphoreType.DMA((3,)),
            pltpu.SemaphoreType.DMA((SIDE,)),
            pltpu.SemaphoreType.DMA((4,)),
            pltpu.SemaphoreType.DMA((SIDE,)),
            pltpu.SemaphoreType.DMA((SIDE,)),
            pltpu.SemaphoreType.DMA((SIDE, 2)),
            pltpu.SemaphoreType.DMA((SIDE, 2)),
            pltpu.SemaphoreType.DMA((SIDE, tiles)),
            pltpu.SemaphoreType.DMA((2, tiles)),
            pltpu.SemaphoreType.DMA((2, tiles)),
        ],
        compiler_params=pltpu.CompilerParams(
            collective_id=0, has_side_effects=True, vmem_limit_bytes=62 << 20
        ),
    )(
        doc_lengths, queries, key_rows, value_rows, short_taps,
        bypass.reshape(1, width), decay_rate.T, residue.T, out_weight,
    )


def solution(mesh):
    square = mesh.shape["ctx"] == SIDE and mesh.shape["chan"] == SIDE
    return jax.shard_map(
        fused if square else local,
        mesh=mesh,
        in_specs=(
            P(("groups", "ctx"), "chan"),
            P(("groups", "ctx"), "chan"),
            P(("groups", "ctx"), "chan"),
            P(None, None, "chan"),
            P("chan"),
            P("chan", None),
            P("chan", None),
            P("ctx", "chan"),
            P("groups"),
        ),
        out_specs=P(("groups", "ctx"), "chan"),
        check_vma=False,
    )
```

```python
import functools

import jax
import jax.numpy as jnp
from jax import lax
from jax.experimental import pallas as pl
from jax.experimental.pallas import tpu as pltpu
from jax.sharding import PartitionSpec as P

F32 = jnp.float32
BF16 = jnp.bfloat16
SIDE = 4
LANES = 512


def from_behind(value, axis, by):
    length = lax.axis_size(axis)
    pairs = [(i, i + by) for i in range(length) if 0 <= i + by < length]
    return lax.ppermute(value, axis, pairs)


def doc_index(doc_starts, positions):
    return jnp.sum((doc_starts[None, :] <= positions[:, None]).astype(jnp.int32), axis=1) - 1


def local(
    queries, key_rows, value_rows, short_taps, bypass, decay_rate, residue, out_weight, doc_lengths
):
    row_count, width_local = queries.shape
    filt_count, mode_count = decay_rate.shape
    group_size = width_local // filt_count
    dev_index = lax.axis_index("ctx")
    first_row = dev_index * row_count
    highest = lax.Precision.HIGHEST
    stacked = jnp.stack([queries, key_rows, value_rows])
    previous = from_behind(stacked[:, row_count - 2 :, :], "ctx", 1)
    extended = jnp.concatenate([previous, stacked], axis=1)
    filtered = (
        short_taps[:, 0, None, :] * extended[:, 2:, :]
        + short_taps[:, 1, None, :] * extended[:, 1:-1, :]
        + short_taps[:, 2, None, :] * extended[:, :-2, :]
    )
    query_conv = filtered[0]
    gated_input = filtered[1] * filtered[2]
    order = jnp.arange(doc_lengths.shape[0], dtype=jnp.int32)
    before = order[None, :] < order[:, None]
    doc_starts = jnp.sum(jnp.where(before, doc_lengths[None, :], 0), axis=1)
    own_positions = first_row - 1 + jnp.arange(row_count + 1, dtype=jnp.int32)
    docs_ext = doc_index(doc_starts, own_positions)
    doc_in = docs_ext[0]
    rate_t = decay_rate.T
    gain_t = (residue * jnp.sqrt(-jnp.expm1(-2.0 * decay_rate))).T
    block_len = min(128, row_count)
    lag_steps = jnp.arange(block_len, dtype=jnp.float32)
    lag_table = jnp.sum(
        gain_t[:, :, None] * jnp.exp(-rate_t[:, :, None] * lag_steps[None, None, :]), axis=0
    )
    lag_grid = jnp.arange(block_len)[:, None] - jnp.arange(block_len)[None, :]
    causal = lag_grid >= 0
    kernel = jnp.where(causal[None], lag_table[:, jnp.clip(lag_grid, 0, block_len - 1)], 0.0)
    end_weights = jnp.exp(-rate_t[:, :, None] * (block_len - 1.0 - lag_steps[None, None, :]))
    carry_table = gain_t[None, :, :] * jnp.exp(
        -rate_t[None, :, :] * (lag_steps[:, None, None] + 1.0)
    )
    full_decay = jnp.exp(-rate_t * block_len)
    local_starts = []
    local_state = jnp.zeros((mode_count, filt_count, group_size), jnp.float32)
    transfer = jnp.ones((mode_count, filt_count), jnp.float32)
    step = 0
    sub_rows = gated_input.reshape(block_len, filt_count, group_size)
    sub_docs = docs_ext[1 + step * block_len : 1 + (step + 1) * block_len]
    doc_before = docs_ext[step * block_len]
    same_doc = (sub_docs[:, None] == sub_docs[None, :]).astype(jnp.float32)
    masked = kernel * same_doc[None]
    intra_parts = [jnp.einsum("fij,jfg->ifg", masked, sub_rows, precision=highest)]
    last_mask = (sub_docs == sub_docs[-1]).astype(jnp.float32)
    end_state = jnp.einsum(
        "sfj,jfg->sfg", end_weights * last_mask[None, None, :], sub_rows, precision=highest
    )
    carry_masks = [(sub_docs == doc_before).astype(jnp.float32)]
    local_starts.append(local_state)
    transfer_starts = [transfer]
    step_decay = full_decay * (sub_docs[-1] == doc_before).astype(jnp.float32)
    local_state = step_decay[:, :, None] * local_state + end_state
    piece = lax.all_gather(local_state[None], "ctx", axis=0, tiled=True)
    count = piece.shape[0]
    source = jnp.arange(count, dtype=jnp.int32)
    end_docs = doc_index(doc_starts, (source + 1) * row_count - 1)
    valid = ((source < dev_index) & (end_docs == doc_in)).astype(jnp.float32)
    distance = jnp.maximum(dev_index - 1 - source, 0).astype(jnp.float32) * row_count
    factor = jnp.exp(-rate_t[None] * distance[:, None, None]) * valid[:, None, None]
    incoming = jnp.sum(factor[..., None] * piece, axis=0)
    step = 0
    state_start = transfer_starts[step][:, :, None] * incoming
    carried = jnp.einsum("isf,sfg->ifg", carry_table, state_start, precision=highest)
    total = intra_parts[step] + carried * carry_masks[step][:, None, None]
    conv_parts = total.reshape(block_len, width_local)
    mixed = (query_conv * (conv_parts + bypass * gated_input)).astype(jnp.bfloat16)
    weight_full = lax.all_gather(out_weight, "ctx", axis=0, tiled=True)
    projected = jnp.dot(
        lax.all_gather(mixed, "chan", axis=1, tiled=True),
        weight_full,
        preferred_element_type=jnp.float32,
    )
    return projected.astype(jnp.bfloat16)


def fused_kernel(
    docs_ref, q_hbm, k_hbm, v_hbm, taps_hbm, bypass_hbm, rates_ref, residues_ref, w_hbm, out_ref,
    q_ref, k_ref, v_ref, taps_ref, bypass_ref, in_sem,
    w_ref, halo_out, halo_in, ext, u_ref, um_ref, qc_ref, keep_ref, last_ref,
    rate_ref, gain_ref, fac_ref, e_out, e_in, st_ref, prod, mixed, hop_ref, lhs, part,
    own, hold, relay, recv,
    w_sem, halo_sem, e_send, e_recv, t_local, t_send, t_recv,
    hop_sem, x_send, x_recv, s_send, s_recv, rs_send, rs_recv, rl_recv,
):
    c = lax.axis_index("ctx")
    n = lax.axis_index("chan")
    rows, width = q_ref.shape
    modes = rate_ref.shape[0]
    group_size = width // rates_ref.shape[1]
    half = rows // 2
    sib = n + 1 - 2 * lax.rem(n, 2)
    opp = lax.rem(n + 2, SIDE)
    chunks = width // LANES

    def remote(src, dst, send, recv_sem, ctx, chan):
        return pltpu.make_async_remote_copy(
            src_ref=src, dst_ref=dst, send_sem=send, recv_sem=recv_sem,
            device_id={"ctx": ctx, "chan": chan}, device_id_type=pl.DeviceIdType.MESH,
        )

    loads = [
        pltpu.make_async_copy(src, dst, in_sem.at[i])
        for i, (src, dst) in enumerate(
            (
                (q_hbm, q_ref), (k_hbm, k_ref), (v_hbm, v_ref),
                (taps_hbm, taps_ref), (bypass_hbm, bypass_ref),
            )
        )
    ]
    for load in loads:
        load.start()
    load_w = pltpu.make_async_copy(w_hbm, w_ref, w_sem)
    load_w.start()

    barrier = pltpu.get_barrier_semaphore()

    def greet(ctx, chan):
        pl.semaphore_signal(
            barrier, inc=1, device_id={"ctx": ctx, "chan": chan},
            device_id_type=pl.DeviceIdType.MESH,
        )

    for j in range(1, SIDE):
        greet(lax.rem(c + j, SIDE), n)
        greet(c, lax.rem(n + j, SIDE))

    for load in loads:
        load.wait()
    for p, ref in enumerate((q_ref, k_ref, v_ref)):
        halo_out[2 * p : 2 * p + 2, :] = ref[rows - 16 :, :].astype(F32)[14:, :]
    halo_out[6:8, :] = jnp.zeros((2, width), F32)

    @pl.when(c == 0)
    def _():
        halo_in[...] = jnp.zeros_like(halo_in)
        e_in[0] = jnp.zeros_like(e_in[0])

    @pl.when(c <= 1)
    def _():
        e_in[1] = jnp.zeros_like(e_in[1])

    pl.semaphore_wait(barrier, 2 * SIDE - 2)

    halo = remote(halo_out, halo_in, halo_sem.at[0], halo_sem.at[1], lax.rem(c + 1, SIDE), n)

    @pl.when(c < SIDE - 1)
    def _():
        halo.start()

    first = c * rows
    pos = first + lax.broadcasted_iota(jnp.int32, (rows, 128), 0)
    keep = jnp.ones((rows, 128), F32)
    newest = jnp.int32(0)
    crossed = jnp.float32(1.0)
    start = jnp.int32(0)
    for j in range(docs_ref.shape[0]):
        keep = jnp.where(pos == start, 0.0, keep)
        newest = jnp.where(start < first + rows, start, newest)
        inside = jnp.logical_and(start >= first - rows, start < first)
        crossed = jnp.where(inside, jnp.float32(0.0), crossed)
        start = start + docs_ref[j]
    keep_ref[...] = keep
    last_ref[...] = jnp.where(pos >= newest, 1.0, 0.0)

    rate = rates_ref[...]
    twice = 2.0 * rate
    series = jnp.ones_like(twice)
    for term in range(8, 1, -1):
        series = 1.0 - twice * series * (1.0 / term)
    table = jnp.concatenate([rate, residues_ref[...] * jnp.sqrt(twice * series)], axis=0)

    def tables(i, carry):
        lanes = pl.ds(pl.multiple_of(i * LANES, LANES), LANES)
        filt = lax.broadcasted_iota(jnp.int32, (rates_ref.shape[1], LANES), 0)
        chan = lax.broadcasted_iota(jnp.int32, (rates_ref.shape[1], LANES), 1) + i * LANES
        pick = jnp.where(
            jnp.logical_and(chan >= filt * group_size, chan < (filt + 1) * group_size), 1.0, 0.0
        )
        both = jnp.dot(
            table, pick, precision=lax.Precision.HIGHEST, preferred_element_type=F32
        )
        rate_ref[:, lanes] = both[:modes]
        gain_ref[:, lanes] = both[modes:]
        fac_ref[:, lanes] = jnp.exp(-both[:modes])
        return carry

    lax.fori_loop(0, chunks, tables, 0)

    @pl.when(c > 0)
    def _():
        halo.wait_recv()

    def short(i, carry):
        lanes = pl.ds(pl.multiple_of(i * 128, 128), 128)
        convs = []
        for p, ref in enumerate((q_ref, k_ref, v_ref)):
            x = ref[:, lanes].astype(F32)
            ext[p, 8:, :] = x
            ext[p, 6:8, :] = halo_in[2 * p : 2 * p + 2, lanes]
            convs.append(
                taps_ref[p, 0:1, lanes] * x
                + taps_ref[p, 1:2, lanes] * ext[p, 7 : 7 + rows, :]
                + taps_ref[p, 2:3, lanes] * ext[p, 6 : 6 + rows, :]
            )
        u = convs[1] * convs[2]
        qc_ref[:, lanes] = convs[0]
        u_ref[:, lanes] = u
        um_ref[:, lanes] = u * last_ref[...]
        return carry

    lax.fori_loop(0, width // 128, short, 0)

    for part_no in range(2):
        for i in range(chunks // 2):
            at = (part_no * (chunks // 2) + i) * LANES
            lanes = slice(at, at + LANES)
            f0, f1 = fac_ref[0:8, lanes], fac_ref[8:16, lanes]

            def ends(t, state, lanes=lanes, f0=f0, f1=f1):
                s0, s1 = state
                for r in range(8):
                    row = jnp.broadcast_to(um_ref[pl.ds(t * 8 + r, 1), lanes], (8, LANES))
                    s0 = s0 * f0 + row
                    s1 = s1 * f1 + row
                return s0, s1

            zero = jnp.zeros((8, LANES), F32)
            s0, s1 = lax.fori_loop(0, rows // 8, ends, (zero, zero))
            e_out[part_no, :, i * LANES : (i + 1) * LANES] = jnp.concatenate([s0, s1]).astype(BF16)
        for d in (1, 0):

            @pl.when(c + d + 1 < SIDE)
            def _(d=d, part_no=part_no):
                remote(
                    e_out.at[part_no], e_in.at[d, part_no], e_send.at[d, part_no],
                    e_recv.at[d, part_no], lax.rem(c + d + 1, SIDE), n,
                ).start()

    for part_no in range(2):
        for d in range(2):

            @pl.when(c >= d + 1)
            def _(d=d, part_no=part_no):
                remote(
                    e_out.at[part_no], e_in.at[d, part_no], e_send.at[d, part_no],
                    e_recv.at[d, part_no], lax.rem(c + SIDE - d - 1, SIDE), n,
                ).wait_recv()

        part_width = width // 2
        lanes = slice(part_no * part_width, (part_no + 1) * part_width)
        st_ref[:, lanes] = e_in[0, part_no].astype(F32) + (crossed * e_in[1, part_no].astype(F32)) * jnp.exp(
            rate_ref[:, lanes] * (-1.0 * rows)
        )

    def scan_rows(h, first_group, groups):
        for i in range(chunks):
            lanes = slice(i * LANES, (i + 1) * LANES)
            f0, f1 = fac_ref[0:8, lanes], fac_ref[8:16, lanes]
            g0, g1 = gain_ref[0:8, lanes], gain_ref[8:16, lanes]

            def sweep(t, state, lanes=lanes, f0=f0, f1=f1, g0=g0, g1=g1):
                s0, s1 = state
                outs = []
                for b in range(2):
                    base = pl.multiple_of(h * half + first_group * 16 + t * 16 + b * 8, 8)
                    for r in range(8):
                        row = jnp.broadcast_to(u_ref[pl.ds(base + r, 1), lanes], (8, LANES))
                        kept = jnp.broadcast_to(keep_ref[pl.ds(base + r, 1), :], (8, 128))
                        kept = jnp.concatenate([kept] * (LANES // 128), axis=1)
                        s0 = (s0 * kept) * f0 + row
                        s1 = (s1 * kept) * f1 + row
                        terms = g0 * s0 + g1 * s1
                        for z in range(LANES // 128):
                            prod[b, z, r * 8 : r * 8 + 8, :] = terms[:, z * 128 : (z + 1) * 128]
                    sums = []
                    for z in range(LANES // 128):
                        acc = prod[b, z, pl.ds(0, 8, stride=8), :]
                        for m in range(1, 8):
                            acc = acc + prod[b, z, pl.ds(m, 8, stride=8), :]
                        sums.append(acc)
                    conv = jnp.concatenate(sums, axis=1)
                    outs.append(
                        qc_ref[pl.ds(base, 8), lanes]
                        * (conv + bypass_ref[:, lanes] * u_ref[pl.ds(base, 8), lanes])
                    )
                dest = pl.ds(pl.multiple_of(first_group * 16 + t * 16, 16), 16)
                mixed[h, dest, lanes] = jnp.concatenate(outs, axis=0).astype(BF16)
                return s0, s1

            s0, s1 = lax.fori_loop(0, groups, sweep, (st_ref[0:8, lanes], st_ref[8:16, lanes]))
            st_ref[0:8, lanes] = s0
            st_ref[8:16, lanes] = s1

    quarter = half // 2

    def piece(a):
        return slice(a * quarter, (a + 1) * quarter)

    def hop(a):
        return remote(
            mixed.at[0, piece(a)], hop_ref.at[piece(a)], hop_sem.at[a], hop_sem.at[2 + a], c, opp
        )

    def onward_hopped(a, plane):
        return remote(
            hop_ref.at[piece(a)], lhs.at[c, 0, piece(a)], t_send.at[a], t_recv.at[c], plane, n
        )

    def onward(plane):
        return remote(mixed.at[1], lhs.at[c, 1], t_send.at[2], t_recv.at[c], plane, n)

    def stay_hopped(a):
        return pltpu.make_async_copy(
            hop_ref.at[piece(a)], lhs.at[c, 0, piece(a)], t_local.at[a]
        )

    def stay_first():
        return pltpu.make_async_copy(mixed.at[0], lhs.at[c, 0], t_local.at[3])

    def stay():
        return pltpu.make_async_copy(mixed.at[1], lhs.at[c, 1], t_local.at[2])

    groups = half // 16
    scan_rows(0, 0, groups // 2)
    hop(0).start()
    scan_rows(0, groups // 2, groups - groups // 2)
    hop(1).start()
    scan_rows(1, 0, groups)

    @pl.when(n != c)
    def _():
        onward(n).start()

    @pl.when(n == c)
    def _():
        stay().start()
        stay_first().start()

    for a in range(2):
        hop(a).wait_recv()

        @pl.when(opp != c)
        def _(a=a):
            onward_hopped(a, opp).start()

        @pl.when(opp == c)
        def _(a=a):
            stay_hopped(a).start()

    hub = lax.rem(n, 2) == lax.rem(c, 2)
    mine = jnp.where(n == c, 1, 0)
    theirs = 1 - mine

    def arrive(r, k):
        @pl.when(r != c)
        def _():
            remote(
                mixed.at[1], lhs.at[r, k], t_send.at[2], t_recv.at[r], lax.rem(c + 1, SIDE), n
            ).wait_recv()

        @pl.when(r == c)
        def _():
            if k == 1:
                stay().wait()
            else:
                stay_hopped(0).wait()
                stay_hopped(1).wait()

    def across(r, k):
        return remote(lhs.at[r, k], lhs.at[r, k], x_send.at[r], x_recv.at[r], c, opp)

    def hand(r, k):
        return remote(lhs.at[r, k], lhs.at[r, k], s_send.at[r, k], s_recv.at[r, k], c, sib)

    def pass_mine(r):
        @pl.when(hub)
        def _():
            @pl.when(n == c)
            def _():
                arrive(r, 1)

            @pl.when(n != c)
            def _():
                arrive(r, 0)

            @pl.when(jnp.logical_or(n == c, r != c))
            def _():
                across(r, mine).start()

            hand(r, mine).start()

    def pass_theirs(r):
        @pl.when(hub)
        def _():
            @pl.when(jnp.logical_and(n == c, r == c))
            def _():
                stay_first().wait()

            @pl.when(jnp.logical_or(n != c, r != c))
            def _():
                across(r, theirs).wait_recv()

            hand(r, theirs).start()

        @pl.when(jnp.logical_not(hub))
        def _():
            for k in range(2):
                hand(r, k).wait_recv()

    mate = c + 1 - 2 * lax.rem(c, 2)
    end = jnp.logical_or(c == 0, c == SIDE - 1)
    near = jnp.where(c < 2, 2, 1)
    away = jnp.where(c < 2, 3, 0)
    def direct(r, i):
        return remote(part.at[r, i], recv.at[0, i], rs_send.at[r, i], rs_recv.at[0, i], mate, n)

    def crossing(r, i):
        return remote(part.at[r, i], recv.at[1, i], rs_send.at[r, i], rs_recv.at[1, i], r, n)

    def to_relay(r, i):
        slot = lax.rem(r, 2)
        return remote(
            part.at[r, i], relay.at[slot, i], rs_send.at[r, i], rl_recv.at[slot, i], mate, n
        )

    def multiply(r):
        crosses = r // 2 != c // 2

        def tile(i, carry):
            cols = pl.ds(pl.multiple_of(i * LANES, LANES), LANES)
            acc = jnp.dot(
                lhs[r].reshape(rows, width), w_ref[:, cols], preferred_element_type=F32
            )

            @pl.when(r == c)
            def _():
                own[i] = acc

            @pl.when(jnp.logical_and(crosses, jnp.logical_not(end)))
            def _():
                hold[lax.rem(r, 2), i] = acc

            @pl.when(jnp.logical_and(crosses, end))
            def _():
                part[r, i] = acc.astype(BF16)
                to_relay(r, i).start()

            @pl.when(r == mate)
            def _():
                part[r, i] = acc.astype(BF16)

                @pl.when(jnp.logical_or(jnp.logical_not(end), i < 2))
                def _():
                    direct(r, i).start()

            return carry

        lax.fori_loop(0, chunks, tile, 0)

    def add_relayed(r):
        @pl.when(jnp.logical_not(end))
        def _():
            slot = lax.rem(r, 2)

            def tile(i, carry):
                to_relay(r, i).wait_recv()
                part[r, i] = (hold[slot, i] + relay[slot, i].astype(F32)).astype(BF16)
                crossing(r, i).start()
                return carry

            lax.fori_loop(0, chunks, tile, 0)

    load_w.wait()
    pass_mine(c)
    pass_mine(mate)
    pass_theirs(c)
    multiply(c)
    pass_mine(away)
    pass_theirs(mate)
    multiply(mate)
    pass_mine(near)
    pass_theirs(away)
    multiply(away)
    pass_theirs(near)
    add_relayed(away)
    multiply(near)

    @pl.when(end)
    def _():
        for i in range(2, chunks):
            direct(mate, i).start()

    add_relayed(near)

    def finish(i, carry):
        cols = pl.ds(pl.multiple_of(i * LANES, LANES), LANES)
        direct(mate, i).wait_recv()
        total = own[i] + recv[0, i].astype(F32)
        remote(
            part.at[mate, i], recv.at[1, i], rs_send.at[mate, i], rs_recv.at[1, i], mate, n
        ).wait_recv()
        out_ref[:, cols] = (total + recv[1, i].astype(F32)).astype(BF16)
        return carry

    lax.fori_loop(0, chunks, finish, 0)

    @pl.when(c < SIDE - 1)
    def _():
        halo.wait_send()

    for part_no in range(2):
        for d in range(2):

            @pl.when(c + d + 1 < SIDE)
            def _(d=d, part_no=part_no):
                remote(
                    e_out.at[part_no], e_in.at[d, part_no], e_send.at[d, part_no],
                    e_recv.at[d, part_no], lax.rem(c + d + 1, SIDE), n,
                ).wait_send()

    hop(0).wait_send()
    hop(1).wait_send()

    @pl.when(n != c)
    def _():
        onward(n).wait_send()

    @pl.when(opp != c)
    def _():
        onward_hopped(0, opp).wait_send()
        onward_hopped(1, opp).wait_send()

    @pl.when(hub)
    def _():
        for r in range(SIDE):
            @pl.when(jnp.logical_or(n == c, r != c))
            def _(r=r):
                across(r, mine).wait_send()

            for k in range(2):
                hand(r, k).wait_send()

    for j in range(1, SIDE):

        def sent(i, carry, j=j):
            direct(lax.rem(c + j, SIDE), i).wait_send()
            return carry

        lax.fori_loop(0, chunks, sent, 0)


def fused(
    queries, key_rows, value_rows, short_taps, bypass, decay_rate, residue, out_weight, doc_lengths
):
    rows, width = queries.shape
    modes = decay_rate.shape[1]
    vmem = pl.BlockSpec(memory_space=pltpu.VMEM)
    hbm = pl.BlockSpec(memory_space=pltpu.HBM)
    tiles = width // LANES
    block = (rows, LANES)
    return pl.pallas_call(
        fused_kernel,
        out_shape=pltpu.VMEM((rows, width), BF16),
        in_specs=[pl.BlockSpec(memory_space=pltpu.SMEM)] + [hbm] * 5 + [vmem] * 2 + [hbm],
        out_specs=vmem,
        scratch_shapes=[
            pltpu.VMEM((rows, width), BF16),
            pltpu.VMEM((rows, width), BF16),
            pltpu.VMEM((rows, width), BF16),
            pltpu.VMEM((3, 3, width), F32),
            pltpu.VMEM((1, width), F32),
            pltpu.SemaphoreType.DMA((5,)),
            pltpu.VMEM(out_weight.shape, BF16),
            pltpu.VMEM((8, width), F32),
            pltpu.VMEM((8, width), F32),
            pltpu.VMEM((3, rows + 8, 128), F32),
            pltpu.VMEM((rows, width), F32),
            pltpu.VMEM((rows, width), F32),
            pltpu.VMEM((rows, width), F32),
            pltpu.VMEM((rows, 128), F32),
            pltpu.VMEM((rows, 128), F32),
            pltpu.VMEM((modes, width), F32),
            pltpu.VMEM((modes, width), F32),
            pltpu.VMEM((modes, width), F32),
            pltpu.VMEM((2, modes, width // 2), BF16),
            pltpu.VMEM((2, 2, modes, width // 2), BF16),
            pltpu.VMEM((modes, width), F32),
            pltpu.VMEM((2, LANES // 128, 64, 128), F32),
            pltpu.VMEM((2, rows // 2, width), BF16),
            pltpu.VMEM((rows // 2, width), BF16),
            pltpu.VMEM((SIDE, 2, rows // 2, width), BF16),
            pltpu.VMEM((SIDE, tiles) + block, BF16),
            pltpu.VMEM((tiles,) + block, F32),
            pltpu.VMEM((2, tiles) + block, F32),
            pltpu.VMEM((2, tiles) + block, BF16),
            pltpu.VMEM((2, tiles) + block, BF16),
            pltpu.SemaphoreType.DMA,
            pltpu.SemaphoreType.DMA((2,)),
            pltpu.SemaphoreType.DMA((2, 2)),
            pltpu.SemaphoreType.DMA((2, 2)),
            pltpu.SemaphoreType.DMA((4,)),
            pltpu.SemaphoreType.DMA((3,)),
            pltpu.SemaphoreType.DMA((SIDE,)),
            pltpu.SemaphoreType.DMA((4,)),
            pltpu.SemaphoreType.DMA((SIDE,)),
            pltpu.SemaphoreType.DMA((SIDE,)),
            pltpu.SemaphoreType.DMA((SIDE, 2)),
            pltpu.SemaphoreType.DMA((SIDE, 2)),
            pltpu.SemaphoreType.DMA((SIDE, tiles)),
            pltpu.SemaphoreType.DMA((2, tiles)),
            pltpu.SemaphoreType.DMA((2, tiles)),
        ],
        compiler_params=pltpu.CompilerParams(
            collective_id=0, has_side_effects=True, vmem_limit_bytes=62 << 20
        ),
    )(
        doc_lengths, queries, key_rows, value_rows, short_taps,
        bypass.reshape(1, width), decay_rate.T, residue.T, out_weight,
    )


def solution(mesh):
    square = mesh.shape["ctx"] == SIDE and mesh.shape["chan"] == SIDE
    return jax.shard_map(
        fused if square else local,
        mesh=mesh,
        in_specs=(
            P(("groups", "ctx"), "chan"),
            P(("groups", "ctx"), "chan"),
            P(("groups", "ctx"), "chan"),
            P(None, None, "chan"),
            P("chan"),
            P("chan", None),
            P("chan", None),
            P("ctx", "chan"),
            P("groups"),
        ),
        out_specs=P(("groups", "ctx"), "chan"),
        check_vma=False,
    )
```
